32 devices in a mesh: dp: 4 (over y, core), tensor: 8 (over z, x).
Axes of the slice: x: 2, y: 2, z: 4, core: 2. Of those that a mesh axis runs over, the one named last changes fastest.
Arguments:
- inputs: bfloat16 [16384, 28672], P('dp', 'tensor'), may hold values from -6 to 6
- out_grads: bfloat16 [16384, 8192], P('dp', 'tensor'), may hold values from -6 to 6
- proj_in: bfloat16 [28672, 64], P('tensor'), may hold values from -0.03125 to 0.03125
- proj_out: bfloat16 [8192, 64], P('tensor'), may hold values from -0.0625 to 0.0625
- lengths: int32 [16], replicated, may hold values from 1 to 4096, 16384 in all
- valid_feats: bfloat16 [4096, 4096], P('dp', 'tensor'), may hold values from -6 to 6
Outputs:
- scores: float32 [16, 4096], P(None, ('dp', 'tensor'))
The draws below stay inside these ranges and needn't reach their ends.
Inputs may be any that keep to these rules, and one draw needn't show every extreme that they name: The lengths sum to 16384; the largest is exactly 4096.
All inputs are finite; a program needn't handle non-finite values.
Results may differ from the reference program's by a relative error of at most 0.003.
Values sent between devices are 32-bit elements; how exact they have to be, the bound alone decides.
No kernel may reach another device: no remote copies, remote signals or barrier semaphores. Data moves between devices by JAX's collectives and lax.ppermute only.
A program may use at most 128 MiB of HBM per device.

```python
import math
import jax
import jax.numpy as jnp
import numpy as np
from jax import lax

D = 8192
FF = 28672
RANK = 64
PROMPTS = 16
FEAT = 4096
TOKENS = 16384
NVAL = 4096


def block_scale(rng, dims, pieces, least, largest):
    def one(dim, parts):
        steps = jax.random.uniform(jax.random.fold_in(jax.random.fold_in(rng, 6), dim), (parts,), jnp.float32, least / len(pieces), largest / len(pieces))
        return jnp.repeat(jnp.exp(steps), dims[dim] // parts).reshape((-1,) + (1,) * (len(dims) - dim - 1))

    loudness = one(*pieces[0])
    for cut in pieces[1:]:
        loudness = loudness * one(*cut)
    return loudness


def split_up(count, total, bound, skew):
    loads = [(1 << 20) // math.isqrt(rank ** skew) + 1 for rank in range(2, count + 1)]
    spare, counts = total - bound - (count - 1), [1] * (count - 1)
    while spare > 0:
        movable = [i for i in range(count - 1) if counts[i] < bound]
        whole, remaining = sum([loads[i] for i in movable]), spare
        for i in movable:
            addition = min(bound - counts[i], max(1, remaining * loads[i] // whole), spare)
            counts[i] = counts[i] + addition
            spare = spare - addition
    return np.array([bound] + counts)


def ragged_sizes(rng, amount, total, most, skew):
    if amount == 2:
        one = jax.random.randint(rng, (), max(1, total - most), min(most, total - 1) + 1)
        return jnp.stack([one, total - one])
    sizes = jnp.asarray(split_up(amount, total, most, skew), jnp.int32)
    twos = (amount - 1) // 2
    giver, taker = sizes[1:1 + 2 * twos:2], sizes[2:2 + 2 * twos:2]
    margin = jnp.minimum(giver - 1, most - taker)
    shifted = jax.random.randint(jax.random.fold_in(rng, 1), (twos,), 0, 1 << 20) % (margin + 1)
    sizes = sizes.at[1:1 + 2 * twos:2].set(giver - shifted).at[2:2 + 2 * twos:2].set(taker + shifted)
    return sizes[jax.random.permutation(jax.random.fold_in(rng, 2), amount)]


def noise(stream_key, dims, deviation, most, pieces=(), held_as=jnp.bfloat16):
    loudness = block_scale(stream_key, dims, pieces, -0.22, 0.18) if pieces else 1.0
    result = jax.random.normal(stream_key, dims, jnp.float32) * deviation * loudness
    return jnp.minimum(jnp.maximum(result, -most), most).astype(held_as)


def setup_inputs(seed: int = 0) -> dict:
    seeds = jax.random.split(jax.random.key(seed), 7)
    inputs = noise(seeds[0], (TOKENS, FF), 1.0, 6.0, ((0, 4), (1, 8)))
    out_grads = noise(seeds[1], (TOKENS, D), 1.0, 6.0, ((0, 4), (1, 8)))
    proj_in = noise(seeds[2], (FF, RANK), FF ** -0.5, 0.03125, ((0, 8),))
    proj_out = noise(seeds[3], (D, RANK), D ** -0.5, 0.0625, ((0, 8),))
    lengths = ragged_sizes(seeds[4], PROMPTS, TOKENS, TOKENS // 4, 2).astype(jnp.int32)
    valid_feats = noise(seeds[5], (NVAL, FEAT), 1.0, 6.0, ((0, 4), (1, 8)))
    return dict(inputs=inputs, out_grads=out_grads, proj_in=proj_in, proj_out=proj_out, lengths=lengths, valid_feats=valid_feats)


def reference(inputs, out_grads, proj_in, proj_out, lengths, valid_feats):
    act_proj = jnp.dot(inputs, proj_in, preferred_element_type=jnp.float32)
    grad_proj = jnp.dot(out_grads, proj_out, preferred_element_type=jnp.float32)
    prompt_ends = jnp.cumsum(lengths).astype(jnp.int32)
    prompt_starts = (prompt_ends - lengths).astype(jnp.int32)
    positions = jnp.arange(TOKENS, dtype=jnp.int32)

    def prompt_gram(prompt):
        member = ((positions >= prompt_starts[prompt]) & (positions < prompt_ends[prompt])).astype(jnp.float32)
        weighted = grad_proj * member[:, None]
        return jnp.dot(weighted.T, act_proj, precision=lax.Precision.HIGHEST)

    gram_all = lax.map(prompt_gram, jnp.arange(PROMPTS, dtype=jnp.int32))
    gram_all = gram_all.reshape(PROMPTS, RANK * RANK)
    features = (gram_all / lengths[:, None].astype(jnp.float32)).astype(jnp.bfloat16)
    return lax.dot_general(features, valid_feats, (((1,), (1,)), ((), ())), preferred_element_type=jnp.float32)
```

```python
import functools
import math

import jax
import jax.numpy as jnp
from jax import lax
from jax.experimental import pallas as pl
from jax.experimental.pallas import tpu as pltpu
from jax.sharding import PartitionSpec as P

NT = (((1,), (1,)), ((), ()))
VMEM_LIMIT = 24 << 20


def dot_nt(a, b):
    return lax.dot_general(a, b, NT, preferred_element_type=jnp.float32)


def lowest(j):
    return (j & -j).bit_length() - 1


def project_kernel(first, final, n_recv, n_blocks, here, after, me, x, g, *refs):
    refs = list(refs)
    ins = [refs.pop(0) for _ in range(2 if first else 4)]
    recvs = [refs.pop(0) for _ in range(n_recv)]
    out = refs.pop(0)
    nexts = [] if final else [refs.pop(0), refs.pop(0)]
    copies, sem = [], refs.pop()

    def rows(at):
        block, size, offset, count = at
        start = (block ^ (me[0] & (n_blocks - 1))) * size + offset
        return pl.ds(pl.multiple_of(start, math.gcd(size, offset, count)), count)

    def fetch(source, target):
        copy = pltpu.make_async_copy(source, target, sem.at[len(copies)])
        copy.start()
        copies.append(copy)

    if first:
        w_in, w_out, x_now, g_now = refs
        fetch(ins[0], w_in)
        fetch(ins[1], w_out)
        fetch(x.at[rows(here)], x_now)
        fetch(g.at[rows(here)], g_now)
    else:
        w_in, w_out, x_now, g_now = ins
    needed = len(copies)
    if not final:
        fetch(x.at[rows(after)], nexts[0])
        fetch(g.at[rows(after)], nexts[1])
    for copy in copies[:needed]:
        copy.wait()
    rank = w_in.shape[0]
    half = rank // 2
    kept = me[0] // n_blocks
    act = dot_nt(w_in[...], x_now[...])
    grad = dot_nt(w_out[...], g_now[...])
    total = jnp.zeros((2 * rank, act.shape[1]), jnp.float32)
    for r in recvs:
        total = total + r[...]
    out[half : half + rank] = act if not recvs else act + total[half : half + rank]
    for h in range(2):
        to = pl.multiple_of(jnp.where(kept == h, half + rank, 0), half)
        line = grad[h * half : (h + 1) * half]
        for r in recvs:
            line = line + r[pl.ds(to, half), :]
        out[pl.ds(to, half), :] = line
    for copy in copies[needed:]:
        copy.wait()


def project(me, x, g, held, recvs, here, after, n_blocks):
    first, final = len(held) == 2, after is None
    vmem = pl.BlockSpec(memory_space=pltpu.VMEM)
    hbm = pl.BlockSpec(memory_space=pltpu.HBM)
    smem = pl.BlockSpec(memory_space=pltpu.SMEM)
    rank = held[0].shape[0]
    wide = (x.shape[1], g.shape[1])
    outs = [pltpu.VMEM((2 * rank, here[3]), jnp.float32)]
    if not final:
        outs += [pltpu.VMEM((after[3], w), jnp.bfloat16) for w in wide]
    if first:
        outs += [pltpu.VMEM(h.shape, h.dtype) for h in held]
    scratch = [pltpu.VMEM((here[3], w), jnp.bfloat16) for w in wide] if first else []
    size = here[3] * sum(wide)
    made = pl.pallas_call(
        functools.partial(project_kernel, first, final, len(recvs), n_blocks, here, after),
        in_specs=[smem, hbm, hbm] + [hbm if first else vmem] * len(held) + [vmem] * len(recvs),
        out_specs=[vmem] * len(outs),
        out_shape=outs,
        scratch_shapes=scratch + [pltpu.SemaphoreType.DMA((6,))],
        name=f"project_{here[0]}_{here[2]}",
        cost_estimate=pl.CostEstimate(flops=4 * rank * size, bytes_accessed=2 * size, transcendentals=0),
        compiler_params=pltpu.CompilerParams(vmem_limit_bytes=VMEM_LIMIT),
    )(me, x, g, *held, *recvs)
    made = list(made)
    if first:
        return made[0], [made[3], made[4], made[1], made[2]]
    return made[0], list(held[:2]) + made[1:]


def gram_kernel(n_blocks, here, tok_rows, has_prev, me, lengths, own, recv, *refs):
    levels = n_blocks.bit_length()
    prevs = refs[:levels] if has_prev else ()
    outs, hi_rows, lo_rows = refs[-levels - 2 : -2], refs[-2], refs[-1]
    half = own.shape[0] // 4
    piece = own.shape[1]
    prompts = lengths.shape[0]
    act = own[half : 3 * half] + recv[half:]
    grad = own[3 * half :] + recv[:half]
    act_hi = act.astype(jnp.bfloat16)
    act_lo = (act - act_hi.astype(jnp.float32)).astype(jnp.bfloat16)
    which = me[0] & (n_blocks - 1)
    first = me[1] * tok_rows + which * here[1] + here[2]
    row = lax.broadcasted_iota(jnp.int32, (prompts, piece), 0)
    position = first + lax.broadcasted_iota(jnp.int32, (prompts, piece), 1)
    begin = jnp.zeros((prompts, piece), jnp.int32)
    end = jnp.zeros((prompts, piece), jnp.int32)
    running = jnp.int32(0)
    for p in range(prompts):
        begin = jnp.where(row == p, running, begin)
        running = running + lengths[p]
        end = jnp.where(row == p, running, end)
    member = (position >= begin) & (position < end)
    for i in range(half):
        line = jnp.broadcast_to(grad[i : i + 1], (prompts, piece))
        line = jnp.where(member, line, 0.0)
        line_hi = line.astype(jnp.bfloat16)
        hi_rows[i * prompts : (i + 1) * prompts] = line_hi
        lo_rows[i * prompts : (i + 1) * prompts] = (line - line_hi.astype(jnp.float32)).astype(jnp.bfloat16)
    width = half * prompts // n_blocks
    for j in range(n_blocks):
        start = pl.multiple_of((j ^ which) * width, width)
        hi = hi_rows[pl.ds(start, width), :]
        lo = lo_rows[pl.ds(start, width), :]
        total = dot_nt(act_hi, hi) + (dot_nt(act_lo, hi) + dot_nt(act_hi, lo))
        level = lowest(j) if j else levels - 1
        at = j >> (level + 1) if j else 0
        if has_prev:
            total = total + prevs[level][at]
        outs[level][at] = total


def gram(me, lengths, own, recv, prevs, here, n_blocks, tok_rows):
    levels = n_blocks.bit_length()
    half = own.shape[0] // 4
    piece = own.shape[1]
    prompts = lengths.shape[0]
    width = half * prompts // n_blocks
    counts = [n_blocks >> (b + 1) for b in range(levels - 1)] + [1]
    vmem = pl.BlockSpec(memory_space=pltpu.VMEM)
    smem = pl.BlockSpec(memory_space=pltpu.SMEM)
    return pl.pallas_call(
        functools.partial(gram_kernel, n_blocks, here, tok_rows, bool(prevs)),
        in_specs=[smem, smem] + [vmem] * (2 + len(prevs)),
        out_specs=[vmem] * levels,
        out_shape=[jax.ShapeDtypeStruct((c, 2 * half, width), jnp.float32) for c in counts],
        scratch_shapes=[pltpu.VMEM((half * prompts, piece), jnp.bfloat16)] * 2,
        name=f"gram_{here[2]}",
        cost_estimate=pl.CostEstimate(
            flops=12 * half * half * prompts * piece, bytes_accessed=8 * own.size, transcendentals=0
        ),
        compiler_params=pltpu.CompilerParams(vmem_limit_bytes=VMEM_LIMIT),
    )(me, lengths, own, recv, *prevs)


def score_kernel(n_ranks, me, lengths, own, recv, valid, *outs):
    levels = n_ranks.bit_length()
    prompts = lengths.shape[0]
    turned = (own[...] + recv[...]).T
    rank = turned.shape[1]
    row = lax.broadcasted_iota(jnp.int32, (prompts, rank), 0)
    count = jnp.ones((prompts, rank), jnp.int32)
    for p in range(prompts):
        count = jnp.where(row == p, lengths[p], count)
    count = count.astype(jnp.float32)
    lines = turned.shape[0] // prompts
    features = jnp.concatenate(
        [turned[i * prompts : (i + 1) * prompts] / count for i in range(lines)], axis=1
    ).astype(jnp.bfloat16)
    width = valid.shape[0] // n_ranks
    for j in range(n_ranks):
        start = pl.multiple_of((j ^ me[0]) * width, width)
        level = lowest(j) if j else levels - 1
        at = j >> (level + 1) if j else 0
        outs[level][at] = dot_nt(features, valid[pl.ds(start, width), :])


def score(me, lengths, own, recv, valid, n_ranks):
    levels = n_ranks.bit_length()
    prompts = lengths.shape[0]
    width = valid.shape[0] // n_ranks
    counts = [n_ranks >> (b + 1) for b in range(levels - 1)] + [1]
    vmem = pl.BlockSpec(memory_space=pltpu.VMEM)
    smem = pl.BlockSpec(memory_space=pltpu.SMEM)
    return pl.pallas_call(
        functools.partial(score_kernel, n_ranks),
        in_specs=[smem, smem, vmem, vmem, vmem],
        out_specs=[vmem] * levels,
        out_shape=[jax.ShapeDtypeStruct((c, prompts, width), jnp.float32) for c in counts],
        name="score",
        cost_estimate=pl.CostEstimate(
            flops=2 * prompts * valid.size, bytes_accessed=2 * valid.size, transcendentals=0
        ),
        compiler_params=pltpu.CompilerParams(vmem_limit_bytes=VMEM_LIMIT),
    )(me, lengths, own, recv, valid)


def swap(value, axis, bit):
    count = lax.axis_size(axis)
    return lax.ppermute(value, axis, [(i, i ^ (1 << bit)) for i in range(count)])


def halving(groups, axis):
    for b in range(len(groups) - 1):
        got = swap(groups[b], axis, b)
        groups = list(groups)
        for c in range(b + 1, len(groups) - 1):
            step = 1 << (c - b)
            first = 1 << (c - b - 1)
            groups[c] = groups[c] + got[first::step]
        groups[-1] = groups[-1] + got[:1]
    return groups[-1]


def shards(inputs, out_grads, proj_in, proj_out, lengths, valid_feats):
    tok_rows = inputs.shape[0]
    n_ranks = lax.axis_size("tensor")
    top = n_ranks.bit_length() - 2
    n_blocks = n_ranks // 2
    me = jnp.stack([lax.axis_index("tensor"), lax.axis_index("dp")]).astype(jnp.int32)
    rank = proj_in.shape[1]
    size = tok_rows // n_blocks
    parts = [(0, size // 2), (size // 2, size // 2)]
    x, g, w_in, w_out = (
        pltpu.with_memory_space_constraint(v, pltpu.HBM)
        for v in (inputs, out_grads, proj_in.T, proj_out.T)
    )

    order = sorted(range(1, n_blocks), key=lambda j: (lowest(j), -j))
    pieces = [(j, c) for j in order for c in range(2)]
    if n_blocks == 4:
        pieces = [(3, 0), (3, 1), (1, 0), (2, 0), (1, 1), (2, 1)]
    pieces += [(0, 0), (0, 1)]
    spots = [(j, size, *parts[c]) for j, c in pieces]
    arrived, grams, held = {}, (), [w_in, w_out]
    for n, (j, c) in enumerate(pieces):
        depth = lowest(j) if j else top
        recvs = [arrived[(j | 1 << b, c)] for b in range(depth)]
        after = spots[n + 1] if n + 1 < len(spots) else None
        own, held = project(me, x, g, held, recvs if j else [], spots[n], after, n_blocks)
        if j:
            arrived[(j, c)] = swap(own, "tensor", depth)
        else:
            for r in recvs:
                own = own + r
            other = swap(own[: rank + rank // 2], "tensor", top)
            grams = gram(me, lengths, own, other, grams, spots[n], n_blocks, tok_rows)
    mine = halving(grams, "tensor")[0]
    dp_bits = lax.axis_size("dp").bit_length() - 1
    for b in range(dp_bits - 1):
        mine = mine + swap(mine, "dp", b)
    groups = score(me, lengths, mine, swap(mine, "dp", dp_bits - 1), valid_feats, n_ranks)
    return halving(groups, "tensor")[0]


def solution(mesh):
    return jax.shard_map(
        shards,
        mesh=mesh,
        in_specs=(
            P("dp", "tensor"),
            P("dp", "tensor"),
            P("tensor", None),
            P("tensor", None),
            P(),
            P("dp", "tensor"),
        ),
        out_specs=P(None, ("dp", "tensor")),
        check_vma=False,
    )
```

```python
import functools

import jax
import jax.numpy as jnp
from jax import lax
from jax.experimental import pallas as pl
from jax.experimental.pallas import tpu as pltpu
from jax.sharding import PartitionSpec as P


NT = (((1,), (1,)), ((), ()))
VMEM_LIMIT = 24 << 20
AHEAD = 2


def dot_nt(a, b):
    return lax.dot_general(a, b, NT, preferred_element_type=jnp.float32)


def lowest(j):
    return (j & -j).bit_length() - 1


def project_kernel(first, n_blocks, here, after, me, x, g, w_in, w_out, *refs):
    refs = list(refs)
    sent = (w_in, w_out)
    if not first:
        refs = refs[2:]
    outs = [refs.pop(0) for _ in here]
    ahead = (refs.pop(0), refs.pop(0)) if after else None
    if first:
        w_in, w_out = refs.pop(0), refs.pop(0)
    x_rows, g_rows, sem, end_sem = refs
    strip = x_rows.shape[1]

    def rows(at, i):
        block, size, offset, _ = at
        start = (block ^ (me[0] & (n_blocks - 1))) * size + offset + i * strip
        return pl.ds(pl.multiple_of(start, strip), strip)

    late = []
    if first:
        for k in range(2):
            late.append(pltpu.make_async_copy(sent[k], (w_in, w_out)[k], end_sem.at[k]))
            late[-1].start()
    places = strips_of(here, strip)
    held = 0 if first else ahead_of(here, strip)
    for slot in range(held, len(places)):
        at, i = places[slot]
        pltpu.make_async_copy(x.at[rows(at, i)], x_rows.at[slot], sem.at[slot, 0]).start()
        pltpu.make_async_copy(g.at[rows(at, i)], g_rows.at[slot], sem.at[slot, 1]).start()
    if after:
        for slot in range(ahead_of(after, strip)):
            at, i = strips_of(after, strip)[slot]
            for k, source in enumerate((x, g)):
                copy = pltpu.make_async_copy(
                    source.at[rows(at, i)], ahead[k].at[slot], end_sem.at[2 + 2 * slot + k]
                )
                copy.start()
                late.append(copy)
    if first:
        late.pop(0).wait()
        late.pop(0).wait()

    rank = w_in.shape[0]
    half = rank // 2
    kept = me[0] // n_blocks
    to = [pl.multiple_of(jnp.where(kept == h, half + rank, 0), half) for h in range(2)]

    def body(slot, _):
        @pl.when(slot >= held)
        def _():
            pltpu.make_async_copy(x_rows.at[slot], x_rows.at[slot], sem.at[slot, 0]).wait()
            pltpu.make_async_copy(g_rows.at[slot], g_rows.at[slot], sem.at[slot, 1]).wait()

        act = dot_nt(w_in[...], x_rows[slot])
        grad = dot_nt(w_out[...], g_rows[slot])
        begin = 0
        for out, at in zip(outs, here):
            end = begin + at[3] // strip

            @pl.when((slot >= begin) & (slot < end))
            def _(out=out, begin=begin):
                cols = pl.ds(pl.multiple_of((slot - begin) * strip, strip), strip)
                out[half : half + rank, cols] = act
                for h in range(2):
                    out[pl.ds(to[h], half), cols] = grad[h * half : (h + 1) * half]

            begin = end
        return 0

    lax.fori_loop(0, len(places), body, 0)
    for copy in late:
        copy.wait()


def strips_of(call, strip):
    return [(at, i) for at in call for i in range(at[3] // strip)]


def ahead_of(call, strip):
    return min(AHEAD, len(strips_of(call, strip)))


def project(me, x, g, held, here, after, n_blocks, strip):
    first = len(held) == 2
    vmem = pl.BlockSpec(memory_space=pltpu.VMEM)
    hbm = pl.BlockSpec(memory_space=pltpu.HBM)
    smem = pl.BlockSpec(memory_space=pltpu.SMEM)
    rank = held[0].shape[0]
    wide = (x.shape[1], g.shape[1])
    count = len(here)

    def rows(call):
        return [pltpu.VMEM((len(strips_of(call, strip)), strip, w), jnp.bfloat16) for w in wide]

    outs = [pltpu.VMEM((2 * rank, at[3]), jnp.float32) for at in here]
    if after:
        outs += rows(after)
    if first:
        outs += [pltpu.VMEM(h.shape, h.dtype) for h in held]
        scratch, aliases = rows(here), {}
    else:
        scratch, aliases = [], {5: len(outs), 6: len(outs) + 1}
        outs += rows(here)
    scratch += [
        pltpu.SemaphoreType.DMA((len(strips_of(here, strip)), 2)),
        pltpu.SemaphoreType.DMA((2 + 2 * AHEAD,)),
    ]
    size = sum(at[3] for at in here) * sum(wide)
    made = pl.pallas_call(
        functools.partial(project_kernel, first, n_blocks, here, after),
        in_specs=[smem, hbm, hbm] + [hbm if first else vmem] * len(held),
        out_specs=[vmem] * len(outs),
        out_shape=outs,
        scratch_shapes=scratch,
        input_output_aliases=aliases,
        cost_estimate=pl.CostEstimate(flops=4 * rank * size, bytes_accessed=2 * size, transcendentals=0),
        compiler_params=pltpu.CompilerParams(vmem_limit_bytes=VMEM_LIMIT),
    )(me, x, g, *held)
    made = list(made)
    weights = made[count + 2 : count + 4] if first else list(held[:2])
    return made[:count], weights + made[count : count + 2]


def gram_kernel(n_blocks, here, tok_rows, has_prev, me, lengths, own, recv, *refs):
    levels = n_blocks.bit_length()
    prevs = refs[:levels] if has_prev else ()
    outs, hi_rows, lo_rows = refs[-levels - 2 : -2], refs[-2], refs[-1]
    half = own.shape[0] // 4
    piece = own.shape[1]
    prompts = lengths.shape[0]
    act = own[half : 3 * half] + recv[half:]
    grad = own[3 * half :] + recv[:half]
    act_hi = act.astype(jnp.bfloat16)
    act_lo = (act - act_hi.astype(jnp.float32)).astype(jnp.bfloat16)
    which = me[0] & (n_blocks - 1)
    first = me[1] * tok_rows + which * here[1] + here[2]
    row = lax.broadcasted_iota(jnp.int32, (prompts, piece), 0)
    position = first + lax.broadcasted_iota(jnp.int32, (prompts, piece), 1)
    begin = jnp.zeros((prompts, piece), jnp.int32)
    end = jnp.zeros((prompts, piece), jnp.int32)
    running = jnp.int32(0)
    for p in range(prompts):
        begin = jnp.where(row == p, running, begin)
        running = running + lengths[p]
        end = jnp.where(row == p, running, end)
    member = (position >= begin) & (position < end)
    for i in range(half):
        line = jnp.broadcast_to(grad[i : i + 1], (prompts, piece))
        line = jnp.where(member, line, 0.0)
        line_hi = line.astype(jnp.bfloat16)
        hi_rows[i * prompts : (i + 1) * prompts] = line_hi
        lo_rows[i * prompts : (i + 1) * prompts] = (line - line_hi.astype(jnp.float32)).astype(jnp.bfloat16)
    width = half * prompts // n_blocks
    for j in range(n_blocks):
        start = pl.multiple_of((j ^ which) * width, width)
        hi = hi_rows[pl.ds(start, width), :]
        lo = lo_rows[pl.ds(start, width), :]
        total = dot_nt(act_hi, hi) + (dot_nt(act_lo, hi) + dot_nt(act_hi, lo))
        level = lowest(j) if j else levels - 1
        at = j >> (level + 1) if j else 0
        if has_prev:
            total = total + prevs[level][at]
        outs[level][at] = total


def gram(me, lengths, own, recv, prevs, here, n_blocks, tok_rows):
    levels = n_blocks.bit_length()
    half = own.shape[0] // 4
    piece = own.shape[1]
    prompts = lengths.shape[0]
    width = half * prompts // n_blocks
    counts = [n_blocks >> (b + 1) for b in range(levels - 1)] + [1]
    vmem = pl.BlockSpec(memory_space=pltpu.VMEM)
    smem = pl.BlockSpec(memory_space=pltpu.SMEM)
    return pl.pallas_call(
        functools.partial(gram_kernel, n_blocks, here, tok_rows, bool(prevs)),
        in_specs=[smem, smem] + [vmem] * (2 + len(prevs)),
        out_specs=[vmem] * levels,
        out_shape=[jax.ShapeDtypeStruct((c, 2 * half, width), jnp.float32) for c in counts],
        scratch_shapes=[pltpu.VMEM((half * prompts, piece), jnp.bfloat16)] * 2,
        cost_estimate=pl.CostEstimate(
            flops=12 * half * half * prompts * piece, bytes_accessed=8 * own.size, transcendentals=0
        ),
        compiler_params=pltpu.CompilerParams(vmem_limit_bytes=VMEM_LIMIT),
    )(me, lengths, own, recv, *prevs)


def score_kernel(n_ranks, me, lengths, own, recv, valid, *outs):
    levels = n_ranks.bit_length()
    prompts = lengths.shape[0]
    turned = (own[...] + recv[...]).T
    rank = turned.shape[1]
    row = lax.broadcasted_iota(jnp.int32, (prompts, rank), 0)
    count = jnp.ones((prompts, rank), jnp.int32)
    for p in range(prompts):
        count = jnp.where(row == p, lengths[p], count)
    count = count.astype(jnp.float32)
    lines = turned.shape[0] // prompts
    features = jnp.concatenate(
        [turned[i * prompts : (i + 1) * prompts] / count for i in range(lines)], axis=1
    ).astype(jnp.bfloat16)
    width = valid.shape[0] // n_ranks
    for j in range(n_ranks):
        start = pl.multiple_of((j ^ me[0]) * width, width)
        level = lowest(j) if j else levels - 1
        at = j >> (level + 1) if j else 0
        outs[level][at] = dot_nt(features, valid[pl.ds(start, width), :])


def score(me, lengths, own, recv, valid, n_ranks):
    levels = n_ranks.bit_length()
    prompts = lengths.shape[0]
    width = valid.shape[0] // n_ranks
    counts = [n_ranks >> (b + 1) for b in range(levels - 1)] + [1]
    vmem = pl.BlockSpec(memory_space=pltpu.VMEM)
    smem = pl.BlockSpec(memory_space=pltpu.SMEM)
    return pl.pallas_call(
        functools.partial(score_kernel, n_ranks),
        in_specs=[smem, smem, vmem, vmem, vmem],
        out_specs=[vmem] * levels,
        out_shape=[jax.ShapeDtypeStruct((c, prompts, width), jnp.float32) for c in counts],
        name="score",
        cost_estimate=pl.CostEstimate(
            flops=2 * prompts * valid.size, bytes_accessed=2 * valid.size, transcendentals=0
        ),
        compiler_params=pltpu.CompilerParams(vmem_limit_bytes=VMEM_LIMIT),
    )(me, lengths, own, recv, valid)


def swap(value, axis, bit):
    count = lax.axis_size(axis)
    return lax.ppermute(value, axis, [(i, i ^ (1 << bit)) for i in range(count)])


def halving(groups, axis):
    for b in range(len(groups) - 1):
        got = swap(groups[b], axis, b)
        groups = list(groups)
        for c in range(b + 1, len(groups) - 1):
            step = 1 << (c - b)
            first = 1 << (c - b - 1)
            groups[c] = groups[c] + got[first::step]
        groups[-1] = groups[-1] + got[:1]
    return groups[-1]


def plan(n_blocks):
    if n_blocks == 4:
        return [[(3, 0)], [(3, 1), (1, 0), (2, 0)], [(2, 1), (1, 1), (0, 0)], [(0, 1)]]
    order = sorted(range(1, n_blocks), key=lambda j: (lowest(j), -j))
    return [[(j, 0), (j, 1)] for j in order] + [[(0, 0), (0, 1)]]


def shards(inputs, out_grads, proj_in, proj_out, lengths, valid_feats):
    tok_rows = inputs.shape[0]
    n_ranks = lax.axis_size("tensor")
    top = n_ranks.bit_length() - 2
    n_blocks = n_ranks // 2
    me = jnp.stack([lax.axis_index("tensor"), lax.axis_index("dp")]).astype(jnp.int32)
    rank = proj_in.shape[1]
    size = tok_rows // n_blocks
    parts = [(0, size // 2), (size // 2, size // 2)]
    strip = min(256, size // 2)
    x, g, w_in, w_out = (
        pltpu.with_memory_space_constraint(v, pltpu.HBM)
        for v in (inputs, out_grads, proj_in.T, proj_out.T)
    )

    calls = plan(n_blocks)
    spots = [[(j, size, *parts[c]) for j, c in call] for call in calls]
    arrived, grams, held = {}, (), [w_in, w_out]
    for n, call in enumerate(calls):
        after = spots[n + 1] if n + 1 < len(spots) else None
        made, held = project(me, x, g, held, spots[n], after, n_blocks, strip)
        for (j, c), own, spot in zip(call, made, spots[n]):
            depth = lowest(j) if j else top
            for b in range(depth):
                own = own + arrived[(j | 1 << b, c)]
            if j:
                arrived[(j, c)] = swap(own, "tensor", depth)
            else:
                other = swap(own[: rank + rank // 2], "tensor", top)
                grams = gram(me, lengths, own, other, grams, spot, n_blocks, tok_rows)
    mine = halving(grams, "tensor")[0]
    dp_bits = lax.axis_size("dp").bit_length() - 1
    for b in range(dp_bits - 1):
        mine = mine + swap(mine, "dp", b)
    groups = score(me, lengths, mine, swap(mine, "dp", dp_bits - 1), valid_feats, n_ranks)
    return halving(groups, "tensor")[0]


def solution(mesh):
    def program(inputs, *rest):
        run = jax.shard_map(
            shards,
            mesh=mesh,
            in_specs=(
                P("dp", "tensor"),
                P("dp", "tensor"),
                P("tensor", None),
                P("tensor", None),
                P(),
                P("dp", "tensor"),
            ),
            out_specs=P(None, ("dp", "tensor")),
            check_vma=False,
        )
        return run(inputs, *rest)

    return program
```

```python
import functools
import math

import jax
import jax.numpy as jnp
from jax import lax
from jax.experimental import pallas as pl
from jax.experimental.pallas import tpu as pltpu
from jax.sharding import PartitionSpec as P


NT = (((1,), (1,)), ((), ()))
VMEM_LIMIT = 24 << 20
AHEAD = 1
CUT = (1, 2)
GRAM_LAST = 1
SCORE_LAST = 0


def dot_nt(a, b):
    return lax.dot_general(a, b, NT, preferred_element_type=jnp.float32)


def place(j, last):
    level = min(lowest(j) if j else last, last)
    return level, j >> (level + 1) if level < last else j >> last


def lowest(j):
    return (j & -j).bit_length() - 1


def project_kernel(first, n_blocks, here, after, me, x, g, w_in, w_out, *refs):
    refs = list(refs)
    sent = (w_in, w_out)
    if not first:
        refs = refs[2:]
    outs = [refs.pop(0) for _ in here]
    ahead = (refs.pop(0), refs.pop(0)) if after else None
    if first:
        w_in, w_out = refs.pop(0), refs.pop(0)
    x_rows, g_rows, sem, end_sem = refs
    strip = x_rows.shape[1]

    def rows(at, i):
        block, size, offset, _ = at
        start = (block ^ (me[0] & (n_blocks - 1))) * size + offset + i * strip
        return pl.ds(pl.multiple_of(start, strip), strip)

    late = []
    if first:
        for k in range(2):
            late.append(pltpu.make_async_copy(sent[k], (w_in, w_out)[k], end_sem.at[k]))
            late[-1].start()
    places = strips_of(here, strip)
    held = 0 if first else ahead_of(here, strip)
    for slot in range(held, len(places)):
        at, i = places[slot]
        pltpu.make_async_copy(x.at[rows(at, i)], x_rows.at[slot], sem.at[slot, 0]).start()
        pltpu.make_async_copy(g.at[rows(at, i)], g_rows.at[slot], sem.at[slot, 1]).start()
    if after:
        for slot in range(ahead_of(after, strip)):
            at, i = strips_of(after, strip)[slot]
            for k, source in enumerate((x, g)):
                copy = pltpu.make_async_copy(
                    source.at[rows(at, i)], ahead[k].at[slot], end_sem.at[2 + 2 * slot + k]
                )
                copy.start()
                late.append(copy)
    if first:
        late.pop(0).wait()
        late.pop(0).wait()

    rank = w_in.shape[0]
    half = rank // 2
    kept = me[0] // n_blocks
    to = [pl.multiple_of(jnp.where(kept == h, half + rank, 0), half) for h in range(2)]

    def body(slot, _):
        @pl.when(slot >= held)
        def _():
            pltpu.make_async_copy(x_rows.at[slot], x_rows.at[slot], sem.at[slot, 0]).wait()
            pltpu.make_async_copy(g_rows.at[slot], g_rows.at[slot], sem.at[slot, 1]).wait()

        act = dot_nt(w_in[...], x_rows[slot])
        grad = dot_nt(w_out[...], g_rows[slot])
        begin = 0
        for out, at in zip(outs, here):
            end = begin + at[3] // strip

            @pl.when((slot >= begin) & (slot < end))
            def _(out=out, begin=begin):
                cols = pl.ds(pl.multiple_of((slot - begin) * strip, strip), strip)
                out[half : half + rank, cols] = act
                for h in range(2):
                    out[pl.ds(to[h], half), cols] = grad[h * half : (h + 1) * half]

            begin = end
        return 0

    lax.fori_loop(0, len(places), body, 0)
    for copy in late:
        copy.wait()


def strips_of(call, strip):
    return [(at, i) for at in call for i in range(at[3] // strip)]


def ahead_of(call, strip):
    return min(AHEAD, len(strips_of(call, strip)))


def project(me, x, g, held, here, after, n_blocks, strip):
    first = len(held) == 2
    vmem = pl.BlockSpec(memory_space=pltpu.VMEM)
    hbm = pl.BlockSpec(memory_space=pltpu.HBM)
    smem = pl.BlockSpec(memory_space=pltpu.SMEM)
    rank = held[0].shape[0]
    wide = (x.shape[1], g.shape[1])
    count = len(here)

    def rows(call):
        return [pltpu.VMEM((len(strips_of(call, strip)), strip, w), jnp.bfloat16) for w in wide]

    outs = [pltpu.VMEM((2 * rank, at[3]), jnp.float32) for at in here]
    if after:
        outs += rows(after)
    if first:
        outs += [pltpu.VMEM(h.shape, h.dtype) for h in held]
        scratch, aliases = rows(here), {}
    else:
        scratch, aliases = [], {5: len(outs), 6: len(outs) + 1}
        outs += rows(here)
    scratch += [
        pltpu.SemaphoreType.DMA((len(strips_of(here, strip)), 2)),
        pltpu.SemaphoreType.DMA((2 + 2 * AHEAD,)),
    ]
    size = sum(at[3] for at in here) * sum(wide)
    made = pl.pallas_call(
        functools.partial(project_kernel, first, n_blocks, here, after),
        in_specs=[smem, hbm, hbm] + [hbm if first else vmem] * len(held),
        out_specs=[vmem] * len(outs),
        out_shape=outs,
        scratch_shapes=scratch,
        input_output_aliases=aliases,
        cost_estimate=pl.CostEstimate(flops=4 * rank * size, bytes_accessed=2 * size, transcendentals=0),
        compiler_params=pltpu.CompilerParams(vmem_limit_bytes=VMEM_LIMIT),
    )(me, x, g, *held)
    made = list(made)
    weights = made[count + 2 : count + 4] if first else list(held[:2])
    return made[:count], weights + made[count : count + 2]


def gram_kernel(n_blocks, here, tok_rows, has_prev, me, lengths, own, recv, *refs):
    levels = n_blocks.bit_length() - GRAM_LAST
    prevs = refs[:levels] if has_prev else ()
    outs, hi_rows, lo_rows = refs[-levels - 2 : -2], refs[-2], refs[-1]
    half = own.shape[0] // 4
    piece = own.shape[1]
    prompts = lengths.shape[0]
    act = own[half : 3 * half] + recv[half:]
    grad = own[3 * half :] + recv[:half]
    act_hi = act.astype(jnp.bfloat16)
    act_lo = (act - act_hi.astype(jnp.float32)).astype(jnp.bfloat16)
    which = me[0] & (n_blocks - 1)
    first = me[1] * tok_rows + which * here[1] + here[2]
    row = lax.broadcasted_iota(jnp.int32, (prompts, piece), 0)
    position = first + lax.broadcasted_iota(jnp.int32, (prompts, piece), 1)
    begin = jnp.zeros((prompts, piece), jnp.int32)
    end = jnp.zeros((prompts, piece), jnp.int32)
    running = jnp.int32(0)
    for p in range(prompts):
        begin = jnp.where(row == p, running, begin)
        running = running + lengths[p]
        end = jnp.where(row == p, running, end)
    member = (position >= begin) & (position < end)
    for i in range(half):
        line = jnp.broadcast_to(grad[i : i + 1], (prompts, piece))
        line = jnp.where(member, line, 0.0)
        line_hi = line.astype(jnp.bfloat16)
        hi_rows[i * prompts : (i + 1) * prompts] = line_hi
        lo_rows[i * prompts : (i + 1) * prompts] = (line - line_hi.astype(jnp.float32)).astype(jnp.bfloat16)
    width = half * prompts // n_blocks
    for j in range(n_blocks):
        start = pl.multiple_of((j ^ which) * width, width)
        hi = hi_rows[pl.ds(start, width), :]
        lo = lo_rows[pl.ds(start, width), :]
        total = dot_nt(act_hi, hi) + (dot_nt(act_lo, hi) + dot_nt(act_hi, lo))
        level, at = place(j, levels - 1)
        if has_prev:
            total = total + prevs[level][at]
        outs[level][at] = total


def gram(me, lengths, own, recv, prevs, here, n_blocks, tok_rows):
    levels = n_blocks.bit_length() - GRAM_LAST
    half = own.shape[0] // 4
    piece = own.shape[1]
    prompts = lengths.shape[0]
    width = half * prompts // n_blocks
    counts = [n_blocks >> (b + 1) for b in range(levels - 1)] + [1 << GRAM_LAST]
    vmem = pl.BlockSpec(memory_space=pltpu.VMEM)
    smem = pl.BlockSpec(memory_space=pltpu.SMEM)
    return pl.pallas_call(
        functools.partial(gram_kernel, n_blocks, here, tok_rows, bool(prevs)),
        in_specs=[smem, smem] + [vmem] * (2 + len(prevs)),
        out_specs=[vmem] * levels,
        out_shape=[jax.ShapeDtypeStruct((c, 2 * half, width), jnp.float32) for c in counts],
        scratch_shapes=[pltpu.VMEM((half * prompts, piece), jnp.bfloat16)] * 2,
        cost_estimate=pl.CostEstimate(
            flops=12 * half * half * prompts * piece, bytes_accessed=8 * own.size, transcendentals=0
        ),
        compiler_params=pltpu.CompilerParams(vmem_limit_bytes=VMEM_LIMIT),
    )(me, lengths, own, recv, *prevs)


def score_kernel(n_ranks, me, lengths, own, valid, *outs):
    levels = n_ranks.bit_length() - SCORE_LAST
    prompts = lengths.shape[0]
    turned = own[...].T
    rank = turned.shape[1]
    row = lax.broadcasted_iota(jnp.int32, (prompts, rank), 0)
    count = jnp.ones((prompts, rank), jnp.int32)
    for p in range(prompts):
        count = jnp.where(row == p, lengths[p], count)
    count = count.astype(jnp.float32)
    lines = turned.shape[0] // prompts
    features = jnp.concatenate(
        [turned[i * prompts : (i + 1) * prompts] / count for i in range(lines)], axis=1
    ).astype(jnp.bfloat16)
    width = valid.shape[0] // n_ranks
    for j in range(n_ranks):
        start = pl.multiple_of((j ^ me[0]) * width, width)
        level, at = place(j, levels - 1)
        outs[level][at] = dot_nt(features, valid[pl.ds(start, width), :])


def score(me, lengths, own, valid, n_ranks):
    levels = n_ranks.bit_length() - SCORE_LAST
    prompts = lengths.shape[0]
    width = valid.shape[0] // n_ranks
    counts = [n_ranks >> (b + 1) for b in range(levels - 1)] + [1 << SCORE_LAST]
    vmem = pl.BlockSpec(memory_space=pltpu.VMEM)
    smem = pl.BlockSpec(memory_space=pltpu.SMEM)
    return pl.pallas_call(
        functools.partial(score_kernel, n_ranks),
        in_specs=[smem, smem, vmem, vmem],
        out_specs=[vmem] * levels,
        out_shape=[jax.ShapeDtypeStruct((c, prompts, width), jnp.float32) for c in counts],
        name="score",
        cost_estimate=pl.CostEstimate(
            flops=2 * prompts * valid.size, bytes_accessed=2 * valid.size, transcendentals=0
        ),
        compiler_params=pltpu.CompilerParams(vmem_limit_bytes=VMEM_LIMIT),
    )(me, lengths, own, valid)


def swap(value, axis, bit):
    count = lax.axis_size(axis)
    return lax.ppermute(value, axis, [(i, i ^ (1 << bit)) for i in range(count)])


def halving(groups, axis):
    groups, last = list(groups), len(groups) - 1
    for b in range(last):
        got = swap(groups[b], axis, b)
        for c in range(b + 1, last):
            groups[c] = groups[c] + got[1 << (c - b - 1) :: 1 << (c - b)]
        groups[last] = groups[last] + got[:: 1 << (last - b - 1)]
    return groups[last]


def direct(pieces):
    dp, tensor = lax.axis_size("dp"), lax.axis_size("tensor")
    total = pieces[0][0]
    for value, dp_mask, mask in pieces[1:]:
        move = dp_mask * tensor + mask
        pairs = [(i, i ^ move) for i in range(dp * tensor)]
        total = total + lax.ppermute(value, ("dp", "tensor"), pairs)
    return total


def plan(n_blocks):
    if n_blocks == 4:
        return [[(3, 0)], [(3, 1), (1, 0), (2, 0)], [(2, 1), (1, 1), (0, 0)], [(0, 1)]]
    order = sorted(range(1, n_blocks), key=lambda j: (lowest(j), -j))
    return [[(j, 0), (j, 1)] for j in order] + [[(0, 0), (0, 1)]]


def shards(inputs, out_grads, proj_in, proj_out, lengths, valid_feats):
    tok_rows = inputs.shape[0]
    n_ranks = lax.axis_size("tensor")
    top = n_ranks.bit_length() - 2
    n_blocks = n_ranks // 2
    me = jnp.stack([lax.axis_index("tensor"), lax.axis_index("dp")]).astype(jnp.int32)
    rank = proj_in.shape[1]
    size = tok_rows // n_blocks
    cut = size * CUT[0] // CUT[1]
    parts = [(0, cut), (cut, size - cut)]
    strip = min(256, math.gcd(cut, size))
    x, g, w_in, w_out = (
        pltpu.with_memory_space_constraint(v, pltpu.HBM)
        for v in (inputs, out_grads, proj_in.T, proj_out.T)
    )

    calls = plan(n_blocks)
    spots = [[(j, size, *parts[c]) for j, c in call] for call in calls]
    arrived, grams, held = {}, (), [w_in, w_out]
    for n, call in enumerate(calls):
        after = spots[n + 1] if n + 1 < len(spots) else None
        made, held = project(me, x, g, held, spots[n], after, n_blocks, strip)
        for (j, c), own, spot in zip(call, made, spots[n]):
            depth = lowest(j) if j else top
            for b in range(depth):
                own = own + arrived[(j | 1 << b, c)]
            if j:
                arrived[(j, c)] = swap(own, "tensor", depth)
            else:
                other = swap(own[: rank + rank // 2], "tensor", top)
                grams = gram(me, lengths, own, other, grams, spot, n_blocks, tok_rows)
    kept = halving(grams, "tensor")
    dp_top = lax.axis_size("dp") // 2
    for b in range(dp_top.bit_length() - 1):
        kept = kept + swap(kept, "dp", b)
    if GRAM_LAST:
        z = n_blocks // 2
        mine = direct([(kept[0], 0, 0), (kept[1], 0, z), (kept[0], dp_top, 0), (kept[1], dp_top, z)])
    else:
        mine = direct([(kept[0], 0, 0), (kept[0], dp_top, 0)])
    kept = halving(score(me, lengths, mine, valid_feats, n_ranks), "tensor")
    count = 1 << SCORE_LAST
    return direct([(kept[i], 0, i * (n_ranks // count)) for i in range(count)])


def solution(mesh):
    def program(inputs, *rest):
        run = jax.shard_map(
            shards,
            mesh=mesh,
            in_specs=(
                P("dp", "tensor"),
                P("dp", "tensor"),
                P("tensor", None),
                P("tensor", None),
                P(),
                P("dp", "tensor"),
            ),
            out_specs=P(None, ("dp", "tensor")),
            check_vma=False,
        )
        return run(inputs, *rest)

    return program
```

```python
import functools
import math

import jax
import jax.numpy as jnp
from jax import lax
from jax.experimental import pallas as pl
from jax.experimental.pallas import tpu as pltpu
from jax.sharding import PartitionSpec as P


NT = (((1,), (1,)), ((), ()))
VMEM_LIMIT = 24 << 20
AHEAD = 1
CUT = (1, 2)
GRAM_LAST = 1
SCORE_LAST = 0


def dot_nt(a, b):
    return lax.dot_general(a, b, NT, preferred_element_type=jnp.float32)


def place(j, last):
    level = min(lowest(j) if j else last, last)
    return level, j >> (level + 1) if level < last else j >> last


def lowest(j):
    return (j & -j).bit_length() - 1


def project_kernel(first, n_blocks, here, after, me, x, g, w_in, w_out, *refs):
    refs = list(refs)
    sent = (w_in, w_out)
    if not first:
        refs = refs[2:]
    outs = [refs.pop(0) for _ in here]
    ahead = (refs.pop(0), refs.pop(0)) if after else None
    if first:
        w_in, w_out = refs.pop(0), refs.pop(0)
    x_rows, g_rows, sem, end_sem = refs
    strip = x_rows.shape[1]

    def rows(at, i):
        block, size, offset, _ = at
        start = (block ^ (me[0] & (n_blocks - 1))) * size + offset + i * strip
        return pl.ds(pl.multiple_of(start, strip), strip)

    late = []
    if first:
        for k in range(2):
            late.append(pltpu.make_async_copy(sent[k], (w_in, w_out)[k], end_sem.at[k]))
            late[-1].start()
    places = strips_of(here, strip)
    held = 0 if first else ahead_of(here, strip)
    for slot in range(held, len(places)):
        at, i = places[slot]
        pltpu.make_async_copy(x.at[rows(at, i)], x_rows.at[slot], sem.at[slot, 0]).start()
        pltpu.make_async_copy(g.at[rows(at, i)], g_rows.at[slot], sem.at[slot, 1]).start()
    if after:
        for slot in range(ahead_of(after, strip)):
            at, i = strips_of(after, strip)[slot]
            for k, source in enumerate((x, g)):
                copy = pltpu.make_async_copy(
                    source.at[rows(at, i)], ahead[k].at[slot], end_sem.at[2 + 2 * slot + k]
                )
                copy.start()
                late.append(copy)
    if first:
        late.pop(0).wait()
        late.pop(0).wait()

    rank = w_in.shape[0]
    half = rank // 2
    kept = me[0] // n_blocks
    to = [pl.multiple_of(jnp.where(kept == h, half + rank, 0), half) for h in range(2)]

    def body(slot, _):
        @pl.when(slot >= held)
        def _():
            pltpu.make_async_copy(x_rows.at[slot], x_rows.at[slot], sem.at[slot, 0]).wait()
            pltpu.make_async_copy(g_rows.at[slot], g_rows.at[slot], sem.at[slot, 1]).wait()

        act = dot_nt(w_in[...], x_rows[slot])
        grad = dot_nt(w_out[...], g_rows[slot])
        begin = 0
        for out, at in zip(outs, here):
            end = begin + at[3] // strip

            @pl.when((slot >= begin) & (slot < end))
            def _(out=out, begin=begin):
                cols = pl.ds(pl.multiple_of((slot - begin) * strip, strip), strip)
                out[half : half + rank, cols] = act
                for h in range(2):
                    out[pl.ds(to[h], half), cols] = grad[h * half : (h + 1) * half]

            begin = end
        return 0

    lax.fori_loop(0, len(places), body, 0)
    for copy in late:
        copy.wait()


def strips_of(call, strip):
    return [(at, i) for at in call for i in range(at[3] // strip)]


def ahead_of(call, strip):
    return min(AHEAD, len(strips_of(call, strip)))


def project(me, x, g, held, here, after, n_blocks, strip):
    first = len(held) == 2
    vmem = pl.BlockSpec(memory_space=pltpu.VMEM)
    hbm = pl.BlockSpec(memory_space=pltpu.HBM)
    smem = pl.BlockSpec(memory_space=pltpu.SMEM)
    rank = held[0].shape[0]
    wide = (x.shape[1], g.shape[1])
    count = len(here)

    def rows(call):
        return [pltpu.VMEM((len(strips_of(call, strip)), strip, w), jnp.bfloat16) for w in wide]

    outs = [pltpu.VMEM((2 * rank, at[3]), jnp.float32) for at in here]
    if after:
        outs += rows(after)
    if first:
        outs += [pltpu.VMEM(h.shape, h.dtype) for h in held]
        scratch, aliases = rows(here), {}
    else:
        scratch, aliases = [], {5: len(outs), 6: len(outs) + 1}
        outs += rows(here)
    scratch += [
        pltpu.SemaphoreType.DMA((len(strips_of(here, strip)), 2)),
        pltpu.SemaphoreType.DMA((2 + 2 * AHEAD,)),
    ]
    size = sum(at[3] for at in here) * sum(wide)
    made = pl.pallas_call(
        functools.partial(project_kernel, first, n_blocks, here, after),
        in_specs=[smem, hbm, hbm] + [hbm if first else vmem] * len(held),
        out_specs=[vmem] * len(outs),
        out_shape=outs,
        scratch_shapes=scratch,
        input_output_aliases=aliases,
        cost_estimate=pl.CostEstimate(flops=4 * rank * size, bytes_accessed=2 * size, transcendentals=0),
        compiler_params=pltpu.CompilerParams(vmem_limit_bytes=VMEM_LIMIT),
    )(me, x, g, *held)
    made = list(made)
    weights = made[count + 2 : count + 4] if first else list(held[:2])
    return made[:count], weights + made[count : count + 2]


def gram_kernel(n_blocks, here, tok_rows, has_prev, me, lengths, own, recv, *refs):
    levels = n_blocks.bit_length() - GRAM_LAST
    prevs = refs[:levels] if has_prev else ()
    outs = refs[-levels - 3 : -3]
    hi_rows, lo_rows, placed = refs[-3:]
    half = own.shape[0] // 4
    piece = own.shape[1]
    prompts = lengths.shape[0]
    act = own[half : 3 * half] + recv[half:]
    grad = own[3 * half :] + recv[:half]
    act_hi = act.astype(jnp.bfloat16)
    act_lo = (act - act_hi.astype(jnp.float32)).astype(jnp.bfloat16)
    which = me[0] & (n_blocks - 1)
    first = me[1] * tok_rows + which * here[1] + here[2]
    row = lax.broadcasted_iota(jnp.int32, (prompts, piece), 0)
    position = first + lax.broadcasted_iota(jnp.int32, (prompts, piece), 1)
    begin = jnp.zeros((prompts, piece), jnp.int32)
    end = jnp.zeros((prompts, piece), jnp.int32)
    running = jnp.int32(0)
    for p in range(prompts):
        begin = jnp.where(row == p, running, begin)
        running = running + lengths[p]
        end = jnp.where(row == p, running, end)
    member = (position >= begin) & (position < end)
    for i in range(half):
        line = jnp.broadcast_to(grad[i : i + 1], (prompts, piece))
        line = jnp.where(member, line, 0.0)
        line_hi = line.astype(jnp.bfloat16)
        hi_rows[i * prompts : (i + 1) * prompts] = line_hi
        lo_rows[i * prompts : (i + 1) * prompts] = (line - line_hi.astype(jnp.float32)).astype(jnp.bfloat16)
    width = half * prompts // n_blocks
    both = dot_nt(jnp.concatenate([act_hi, act_lo], axis=0), hi_rows[...])
    sums = both[: 2 * half] + (both[2 * half :] + dot_nt(act_hi, lo_rows[...]))
    for s in range(n_blocks):
        placed[s ^ which] = sums[:, s * width : (s + 1) * width]
    for j in range(n_blocks):
        total = placed[j]
        level, at = place(j, levels - 1)
        if has_prev:
            total = total + prevs[level][at]
        outs[level][at] = total


def gram(me, lengths, own, recv, prevs, here, n_blocks, tok_rows):
    levels = n_blocks.bit_length() - GRAM_LAST
    half = own.shape[0] // 4
    piece = own.shape[1]
    prompts = lengths.shape[0]
    width = half * prompts // n_blocks
    counts = [n_blocks >> (b + 1) for b in range(levels - 1)] + [1 << GRAM_LAST]
    vmem = pl.BlockSpec(memory_space=pltpu.VMEM)
    smem = pl.BlockSpec(memory_space=pltpu.SMEM)
    return pl.pallas_call(
        functools.partial(gram_kernel, n_blocks, here, tok_rows, bool(prevs)),
        in_specs=[smem, smem] + [vmem] * (2 + len(prevs)),
        out_specs=[vmem] * levels,
        out_shape=[jax.ShapeDtypeStruct((c, 2 * half, width), jnp.float32) for c in counts],
        scratch_shapes=[pltpu.VMEM((half * prompts, piece), jnp.bfloat16)] * 2
        + [pltpu.VMEM((n_blocks, 2 * half, width), jnp.float32)],
        cost_estimate=pl.CostEstimate(
            flops=12 * half * half * prompts * piece, bytes_accessed=8 * own.size, transcendentals=0
        ),
        compiler_params=pltpu.CompilerParams(vmem_limit_bytes=VMEM_LIMIT),
    )(me, lengths, own, recv, *prevs)


def score_kernel(n_ranks, me, lengths, own, valid, *outs):
    levels = n_ranks.bit_length() - SCORE_LAST
    prompts = lengths.shape[0]
    turned = own[...].T
    rank = turned.shape[1]
    row = lax.broadcasted_iota(jnp.int32, (prompts, rank), 0)
    count = jnp.ones((prompts, rank), jnp.int32)
    for p in range(prompts):
        count = jnp.where(row == p, lengths[p], count)
    count = count.astype(jnp.float32)
    lines = turned.shape[0] // prompts
    features = jnp.concatenate(
        [turned[i * prompts : (i + 1) * prompts] / count for i in range(lines)], axis=1
    ).astype(jnp.bfloat16)
    width = valid.shape[0] // n_ranks
    for j in range(n_ranks):
        start = pl.multiple_of((j ^ me[0]) * width, width)
        level, at = place(j, levels - 1)
        outs[level][at] = dot_nt(features, valid[pl.ds(start, width), :])


def score(me, lengths, own, valid, n_ranks):
    levels = n_ranks.bit_length() - SCORE_LAST
    prompts = lengths.shape[0]
    width = valid.shape[0] // n_ranks
    counts = [n_ranks >> (b + 1) for b in range(levels - 1)] + [1 << SCORE_LAST]
    vmem = pl.BlockSpec(memory_space=pltpu.VMEM)
    smem = pl.BlockSpec(memory_space=pltpu.SMEM)
    return pl.pallas_call(
        functools.partial(score_kernel, n_ranks),
        in_specs=[smem, smem, vmem, vmem],
        out_specs=[vmem] * levels,
        out_shape=[jax.ShapeDtypeStruct((c, prompts, width), jnp.float32) for c in counts],
        name="score",
        cost_estimate=pl.CostEstimate(
            flops=2 * prompts * valid.size, bytes_accessed=2 * valid.size, transcendentals=0
        ),
        compiler_params=pltpu.CompilerParams(vmem_limit_bytes=VMEM_LIMIT),
    )(me, lengths, own, valid)


def swap(value, axis, bit):
    count = lax.axis_size(axis)
    return lax.ppermute(value, axis, [(i, i ^ (1 << bit)) for i in range(count)])


def halving(groups, axis):
    groups, last = list(groups), len(groups) - 1
    for b in range(last):
        got = swap(groups[b], axis, b)
        for c in range(b + 1, last):
            groups[c] = groups[c] + got[1 << (c - b - 1) :: 1 << (c - b)]
        groups[last] = groups[last] + got[:: 1 << (last - b - 1)]
    return groups[last]


def direct(pieces):
    dp, tensor = lax.axis_size("dp"), lax.axis_size("tensor")
    total = pieces[0][0]
    for value, dp_mask, mask in pieces[1:]:
        move = dp_mask * tensor + mask
        pairs = [(i, i ^ move) for i in range(dp * tensor)]
        total = total + lax.ppermute(value, ("dp", "tensor"), pairs)
    return total


def plan(n_blocks):
    if n_blocks == 4:
        return [[(3, 0)], [(3, 1), (1, 0), (2, 0)], [(2, 1), (1, 1), (0, 0)], [(0, 1)]]
    order = sorted(range(1, n_blocks), key=lambda j: (lowest(j), -j))
    return [[(j, 0), (j, 1)] for j in order] + [[(0, 0), (0, 1)]]


def shards(inputs, out_grads, proj_in, proj_out, lengths, valid_feats):
    tok_rows = inputs.shape[0]
    n_ranks = lax.axis_size("tensor")
    top = n_ranks.bit_length() - 2
    n_blocks = n_ranks // 2
    me = jnp.stack([lax.axis_index("tensor"), lax.axis_index("dp")]).astype(jnp.int32)
    rank = proj_in.shape[1]
    size = tok_rows // n_blocks
    cut = size * CUT[0] // CUT[1]
    parts = [(0, cut), (cut, size - cut)]
    strip = min(256, math.gcd(cut, size))
    x, g, w_in, w_out = (
        pltpu.with_memory_space_constraint(v, pltpu.HBM)
        for v in (inputs, out_grads, proj_in.T, proj_out.T)
    )

    calls = plan(n_blocks)
    spots = [[(j, size, *parts[c]) for j, c in call] for call in calls]
    arrived, grams, held = {}, (), [w_in, w_out]
    for n, call in enumerate(calls):
        after = spots[n + 1] if n + 1 < len(spots) else None
        made, held = project(me, x, g, held, spots[n], after, n_blocks, strip)
        for (j, c), own, spot in zip(call, made, spots[n]):
            depth = lowest(j) if j else top
            for b in range(depth):
                own = own + arrived[(j | 1 << b, c)]
            if j:
                arrived[(j, c)] = swap(own, "tensor", depth)
            else:
                other = swap(own[: rank + rank // 2], "tensor", top)
                grams = gram(me, lengths, own, other, grams, spot, n_blocks, tok_rows)
    kept = halving(grams, "tensor")
    dp_top = lax.axis_size("dp") // 2
    for b in range(dp_top.bit_length() - 1):
        kept = kept + swap(kept, "dp", b)
    if GRAM_LAST:
        z = n_blocks // 2
        mine = direct([(kept[0], 0, 0), (kept[1], 0, z), (kept[0], dp_top, 0), (kept[1], dp_top, z)])
    else:
        mine = direct([(kept[0], 0, 0), (kept[0], dp_top, 0)])
    kept = halving(score(me, lengths, mine, valid_feats, n_ranks), "tensor")
    count = 1 << SCORE_LAST
    return direct([(kept[i], 0, i * (n_ranks // count)) for i in range(count)])


def solution(mesh):
    def program(inputs, *rest):
        run = jax.shard_map(
            shards,
            mesh=mesh,
            in_specs=(
                P("dp", "tensor"),
                P("dp", "tensor"),
                P("tensor", None),
                P("tensor", None),
                P(),
                P("dp", "tensor"),
            ),
            out_specs=P(None, ("dp", "tensor")),
            check_vma=False,
        )
        return run(inputs, *rest)

    return program
```

```python
import functools
import math

import jax
import jax.numpy as jnp
from jax import lax
from jax.experimental import pallas as pl
from jax.experimental.pallas import tpu as pltpu
from jax.sharding import PartitionSpec as P


NT = (((1,), (1,)), ((), ()))
VMEM_LIMIT = 24 << 20
AHEAD = 1
CUT = (1, 2)
GRAM_LAST = 1
SCORE_LAST = 0


def dot_nt(a, b):
    return lax.dot_general(a, b, NT, preferred_element_type=jnp.float32)


def place(j, last):
    level = min(lowest(j) if j else last, last)
    return level, j >> (level + 1) if level < last else j >> last


def lowest(j):
    return (j & -j).bit_length() - 1


def project_kernel(first, n_blocks, here, after, me, x, g, w_in, w_out, *refs):
    refs = list(refs)
    sent = (w_in, w_out)
    if not first:
        refs = refs[2:]
    outs = [refs.pop(0) for _ in here]
    ahead = (refs.pop(0), refs.pop(0)) if after else None
    if first:
        w_in, w_out = refs.pop(0), refs.pop(0)
    x_rows, g_rows, sem, end_sem = refs
    strip = x_rows.shape[1]

    def rows(at, i):
        block, size, offset, _ = at
        start = (block ^ (me[0] & (n_blocks - 1))) * size + offset + i * strip
        return pl.ds(pl.multiple_of(start, strip), strip)

    late = []
    if first:
        for k in range(2):
            late.append(pltpu.make_async_copy(sent[k], (w_in, w_out)[k], end_sem.at[k]))
            late[-1].start()
    places = strips_of(here, strip)
    held = 0 if first else ahead_of(here, strip)
    for slot in range(held, len(places)):
        at, i = places[slot]
        pltpu.make_async_copy(x.at[rows(at, i)], x_rows.at[slot], sem.at[slot, 0]).start()
        pltpu.make_async_copy(g.at[rows(at, i)], g_rows.at[slot], sem.at[slot, 1]).start()
    if after:
        for slot in range(ahead_of(after, strip)):
            at, i = strips_of(after, strip)[slot]
            for k, source in enumerate((x, g)):
                copy = pltpu.make_async_copy(
                    source.at[rows(at, i)], ahead[k].at[slot], end_sem.at[2 + 2 * slot + k]
                )
                copy.start()
                late.append(copy)
    if first:
        late.pop(0).wait()
        late.pop(0).wait()

    rank = w_in.shape[0]
    half = rank // 2
    kept = me[0] // n_blocks
    to = [pl.multiple_of(jnp.where(kept == h, half + rank, 0), half) for h in range(2)]

    def body(slot, _):
        @pl.when(slot >= held)
        def _():
            pltpu.make_async_copy(x_rows.at[slot], x_rows.at[slot], sem.at[slot, 0]).wait()
            pltpu.make_async_copy(g_rows.at[slot], g_rows.at[slot], sem.at[slot, 1]).wait()

        act = dot_nt(w_in[...], x_rows[slot])
        grad = dot_nt(w_out[...], g_rows[slot])
        begin = 0
        for out, at in zip(outs, here):
            end = begin + at[3] // strip

            @pl.when((slot >= begin) & (slot < end))
            def _(out=out, begin=begin):
                cols = pl.ds(pl.multiple_of((slot - begin) * strip, strip), strip)
                out[half : half + rank, cols] = act
                for h in range(2):
                    out[pl.ds(to[h], half), cols] = grad[h * half : (h + 1) * half]

            begin = end
        return 0

    lax.fori_loop(0, len(places), body, 0)
    for copy in late:
        copy.wait()


def strips_of(call, strip):
    return [(at, i) for at in call for i in range(at[3] // strip)]


def ahead_of(call, strip):
    return min(AHEAD, len(strips_of(call, strip)))


def project(me, x, g, held, here, after, n_blocks, strip):
    first = len(held) == 2
    vmem = pl.BlockSpec(memory_space=pltpu.VMEM)
    hbm = pl.BlockSpec(memory_space=pltpu.HBM)
    smem = pl.BlockSpec(memory_space=pltpu.SMEM)
    rank = held[0].shape[0]
    wide = (x.shape[1], g.shape[1])
    count = len(here)

    def rows(call):
        return [pltpu.VMEM((len(strips_of(call, strip)), strip, w), jnp.bfloat16) for w in wide]

    outs = [pltpu.VMEM((2 * rank, at[3]), jnp.float32) for at in here]
    if after:
        outs += rows(after)
    if first:
        outs += [pltpu.VMEM(h.shape, h.dtype) for h in held]
        scratch, aliases = rows(here), {}
    else:
        scratch, aliases = [], {5: len(outs), 6: len(outs) + 1}
        outs += rows(here)
    scratch += [
        pltpu.SemaphoreType.DMA((len(strips_of(here, strip)), 2)),
        pltpu.SemaphoreType.DMA((2 + 2 * AHEAD,)),
    ]
    size = sum(at[3] for at in here) * sum(wide)
    made = pl.pallas_call(
        functools.partial(project_kernel, first, n_blocks, here, after),
        in_specs=[smem, hbm, hbm] + [hbm if first else vmem] * len(held),
        out_specs=[vmem] * len(outs),
        out_shape=outs,
        scratch_shapes=scratch,
        input_output_aliases=aliases,
        cost_estimate=pl.CostEstimate(flops=4 * rank * size, bytes_accessed=2 * size, transcendentals=0),
        compiler_params=pltpu.CompilerParams(vmem_limit_bytes=VMEM_LIMIT),
    )(me, x, g, *held)
    made = list(made)
    weights = made[count + 2 : count + 4] if first else list(held[:2])
    return made[:count], weights + made[count : count + 2]


def gram_kernel(n_blocks, here, tok_rows, has_prev, me, lengths, own, recv, *refs):
    levels = n_blocks.bit_length() - GRAM_LAST
    prevs = refs[:levels] if has_prev else ()
    outs = refs[-levels - 3 : -3]
    hi_rows, lo_rows, placed = refs[-3:]
    half = own.shape[0] // 4
    piece = own.shape[1]
    prompts = lengths.shape[0]
    act = own[half : 3 * half] + recv[half:]
    grad = own[3 * half :] + recv[:half]
    act_hi = act.astype(jnp.bfloat16)
    act_lo = (act - act_hi.astype(jnp.float32)).astype(jnp.bfloat16)
    which = me[0] & (n_blocks - 1)
    first = me[1] * tok_rows + which * here[1] + here[2]
    row = lax.broadcasted_iota(jnp.int32, (prompts, piece), 0)
    position = first + lax.broadcasted_iota(jnp.int32, (prompts, piece), 1)
    begin = jnp.zeros((prompts, piece), jnp.int32)
    end = jnp.zeros((prompts, piece), jnp.int32)
    running = jnp.int32(0)
    for p in range(prompts):
        begin = jnp.where(row == p, running, begin)
        running = running + lengths[p]
        end = jnp.where(row == p, running, end)
    member = (position >= begin) & (position < end)
    for i in range(half):
        line = jnp.broadcast_to(grad[i : i + 1], (prompts, piece))
        line = jnp.where(member, line, 0.0)
        line_hi = line.astype(jnp.bfloat16)
        hi_rows[i * prompts : (i + 1) * prompts] = line_hi
        lo_rows[i * prompts : (i + 1) * prompts] = (line - line_hi.astype(jnp.float32)).astype(jnp.bfloat16)
    width = half * prompts // n_blocks
    both = dot_nt(jnp.concatenate([act_hi, act_lo], axis=0), hi_rows[...])
    sums = both[: 2 * half] + (both[2 * half :] + dot_nt(act_hi, lo_rows[...]))
    for s in range(n_blocks):
        placed[s ^ which] = sums[:, s * width : (s + 1) * width]
    for j in range(n_blocks):
        total = placed[j]
        level, at = place(j, levels - 1)
        if has_prev:
            total = total + prevs[level][at]
        outs[level][at] = total


def gram(me, lengths, own, recv, prevs, here, n_blocks, tok_rows):
    levels = n_blocks.bit_length() - GRAM_LAST
    half = own.shape[0] // 4
    piece = own.shape[1]
    prompts = lengths.shape[0]
    width = half * prompts // n_blocks
    counts = [n_blocks >> (b + 1) for b in range(levels - 1)] + [1 << GRAM_LAST]
    vmem = pl.BlockSpec(memory_space=pltpu.VMEM)
    smem = pl.BlockSpec(memory_space=pltpu.SMEM)
    return pl.pallas_call(
        functools.partial(gram_kernel, n_blocks, here, tok_rows, bool(prevs)),
        in_specs=[smem, smem] + [vmem] * (2 + len(prevs)),
        out_specs=[vmem] * levels,
        out_shape=[jax.ShapeDtypeStruct((c, 2 * half, width), jnp.float32) for c in counts],
        scratch_shapes=[pltpu.VMEM((half * prompts, piece), jnp.bfloat16)] * 2
        + [pltpu.VMEM((n_blocks, 2 * half, width), jnp.float32)],
        cost_estimate=pl.CostEstimate(
            flops=12 * half * half * prompts * piece, bytes_accessed=8 * own.size, transcendentals=0
        ),
        compiler_params=pltpu.CompilerParams(vmem_limit_bytes=VMEM_LIMIT),
    )(me, lengths, own, recv, *prevs)


def score_kernel(n_ranks, me, lengths, own, valid, *refs):
    outs, placed = refs[:-1], refs[-1]
    levels = n_ranks.bit_length() - SCORE_LAST
    prompts = lengths.shape[0]
    turned = own[...].T
    rank = turned.shape[1]
    row = lax.broadcasted_iota(jnp.int32, (prompts, rank), 0)
    count = jnp.ones((prompts, rank), jnp.int32)
    for p in range(prompts):
        count = jnp.where(row == p, lengths[p], count)
    count = count.astype(jnp.float32)
    lines = turned.shape[0] // prompts
    features = jnp.concatenate(
        [turned[i * prompts : (i + 1) * prompts] / count for i in range(lines)], axis=1
    ).astype(jnp.bfloat16)
    width = valid.shape[0] // n_ranks
    sums = dot_nt(features, valid[...])
    for s in range(n_ranks):
        placed[s ^ me[0]] = sums[:, s * width : (s + 1) * width]
    for j in range(n_ranks):
        level, at = place(j, levels - 1)
        outs[level][at] = placed[j]


def score(me, lengths, own, valid, n_ranks):
    levels = n_ranks.bit_length() - SCORE_LAST
    prompts = lengths.shape[0]
    width = valid.shape[0] // n_ranks
    counts = [n_ranks >> (b + 1) for b in range(levels - 1)] + [1 << SCORE_LAST]
    vmem = pl.BlockSpec(memory_space=pltpu.VMEM)
    smem = pl.BlockSpec(memory_space=pltpu.SMEM)
    return pl.pallas_call(
        functools.partial(score_kernel, n_ranks),
        in_specs=[smem, smem, vmem, vmem],
        out_specs=[vmem] * levels,
        out_shape=[jax.ShapeDtypeStruct((c, prompts, width), jnp.float32) for c in counts],
        scratch_shapes=[pltpu.VMEM((n_ranks, prompts, width), jnp.float32)],
        name="score",
        cost_estimate=pl.CostEstimate(
            flops=2 * prompts * valid.size, bytes_accessed=2 * valid.size, transcendentals=0
        ),
        compiler_params=pltpu.CompilerParams(vmem_limit_bytes=VMEM_LIMIT),
    )(me, lengths, own, valid)


def swap(value, axis, bit):
    count = lax.axis_size(axis)
    return lax.ppermute(value, axis, [(i, i ^ (1 << bit)) for i in range(count)])


def halving(groups, axis):
    groups, last = list(groups), len(groups) - 1
    for b in range(last):
        got = swap(groups[b], axis, b)
        for c in range(b + 1, last):
            groups[c] = groups[c] + got[1 << (c - b - 1) :: 1 << (c - b)]
        groups[last] = groups[last] + got[:: 1 << (last - b - 1)]
    return groups[last]


def direct(pieces):
    dp, tensor = lax.axis_size("dp"), lax.axis_size("tensor")
    total = pieces[0][0]
    for value, dp_mask, mask in pieces[1:]:
        move = dp_mask * tensor + mask
        pairs = [(i, i ^ move) for i in range(dp * tensor)]
        total = total + lax.ppermute(value, ("dp", "tensor"), pairs)
    return total


def plan(n_blocks):
    if n_blocks == 4:
        return [[(3, 0)], [(3, 1), (1, 0), (2, 0)], [(2, 1), (1, 1), (0, 0)], [(0, 1)]]
    order = sorted(range(1, n_blocks), key=lambda j: (lowest(j), -j))
    return [[(j, 0), (j, 1)] for j in order] + [[(0, 0), (0, 1)]]


def shards(inputs, out_grads, proj_in, proj_out, lengths, valid_feats):
    tok_rows = inputs.shape[0]
    n_ranks = lax.axis_size("tensor")
    top = n_ranks.bit_length() - 2
    n_blocks = n_ranks // 2
    me = jnp.stack([lax.axis_index("tensor"), lax.axis_index("dp")]).astype(jnp.int32)
    rank = proj_in.shape[1]
    size = tok_rows // n_blocks
    cut = size * CUT[0] // CUT[1]
    parts = [(0, cut), (cut, size - cut)]
    strip = min(256, math.gcd(cut, size))
    x, g, w_in, w_out = (
        pltpu.with_memory_space_constraint(v, pltpu.HBM)
        for v in (inputs, out_grads, proj_in.T, proj_out.T)
    )

    calls = plan(n_blocks)
    spots = [[(j, size, *parts[c]) for j, c in call] for call in calls]
    arrived, grams, held = {}, (), [w_in, w_out]
    for n, call in enumerate(calls):
        after = spots[n + 1] if n + 1 < len(spots) else None
        made, held = project(me, x, g, held, spots[n], after, n_blocks, strip)
        for (j, c), own, spot in zip(call, made, spots[n]):
            depth = lowest(j) if j else top
            for b in range(depth):
                own = own + arrived[(j | 1 << b, c)]
            if j:
                arrived[(j, c)] = swap(own, "tensor", depth)
            else:
                other = swap(own[: rank + rank // 2], "tensor", top)
                grams = gram(me, lengths, own, other, grams, spot, n_blocks, tok_rows)
    kept = halving(grams, "tensor")
    dp_top = lax.axis_size("dp") // 2
    for b in range(dp_top.bit_length() - 1):
        kept = kept + swap(kept, "dp", b)
    if GRAM_LAST:
        z = n_blocks // 2
        mine = direct([(kept[0], 0, 0), (kept[1], 0, z), (kept[0], dp_top, 0), (kept[1], dp_top, z)])
    else:
        mine = direct([(kept[0], 0, 0), (kept[0], dp_top, 0)])
    kept = halving(score(me, lengths, mine, valid_feats, n_ranks), "tensor")
    count = 1 << SCORE_LAST
    return direct([(kept[i], 0, i * (n_ranks // count)) for i in range(count)])


def solution(mesh):
    def program(inputs, *rest):
        run = jax.shard_map(
            shards,
            mesh=mesh,
            in_specs=(
                P("dp", "tensor"),
                P("dp", "tensor"),
                P("tensor", None),
                P("tensor", None),
                P(),
                P("dp", "tensor"),
            ),
            out_specs=P(None, ("dp", "tensor")),
            check_vma=False,
        )
        return run(inputs, *rest)

    return program
```
